32 devices in a mesh: lat: 2 (over core), prop: 16 (over z, y, x).
Axes of the slice: x: 2, y: 2, z: 4, core: 2. Of those that a mesh axis runs over, the one named last changes fastest.
Arguments:
- right_side: float32 [2, 3, 16, 64, 4, 128], P(None, None, None, 'prop', 'lat'), may hold values from -30 to 30
- start_field: float32 [2, 3, 16, 64, 4, 128], P(None, None, None, 'prop', 'lat'), may hold values from -1.75 to 1.75
- region: int32 [64, 4, 128], P('prop', 'lat'), may hold values from 0 to 7
- core_mask: int32 [64, 4, 128], P('prop', 'lat'), may hold values 0 or 1
- intensity: float32 [64, 4, 128], P('prop', 'lat'), may hold values from 0 to 4
- eps_lin: float32 [8], replicated, may hold values from 1 to 12
- eps_loss: float32 [8], replicated, may hold values from 0.1 to 3
- kerr_coef: float32 [8], replicated, may hold values from 0.2 to 1
Outputs:
- new_field: float32 [2, 3, 16, 64, 4, 128], P(None, None, None, 'prop', 'lat')
The draws below stay inside these ranges and needn't reach their ends.
All inputs are finite; a program needn't handle non-finite values. No bound on the sum of `core_mask` on one device may be relied on, other than what follows from the above.
Results may differ from the reference program's by a relative error of at most 0.00002.
Values sent between devices are 32-bit elements; how exact they have to be, the bound alone decides.
A program may use at most 64 MiB of HBM per device.

```python
import math
import jax
import jax.numpy as jnp
from jax import lax

S = 16
NY = 128
NREG = 8
NZ = 64
NX = 4


def draw_right_side(key, part):
    first_key, second_key = jax.random.split(jax.random.fold_in(key, 7))
    full_shape = (2, 3, S, NZ, NX, NY)
    z_fraction = jnp.arange(NZ, dtype=jnp.float32) / max(NZ - 1, 1)
    profile = (1.0 + 2.0 * z_fraction)[:, None, None]
    lateral = jnp.exp(jax.random.uniform(second_key, (NX, NY), jnp.float32, 0.0, math.log(10.0 / 3.0)))
    noise = jnp.clip(jax.random.normal(first_key, full_shape, jnp.float32), -3.0, 3.0)
    return (noise * profile * lateral).astype(jnp.float32)


def with_ends(drawn, own_key, low, largest):
    dims = drawn.shape
    place = [jax.random.randint(jax.random.fold_in(own_key, axis), (), 0, dims[axis]) for axis in range(len(dims))]
    drawn = drawn.at[tuple(place)].set(low)
    longest = dims.index(max(dims))
    place[longest] = (place[longest] + 1) % dims[longest]
    return drawn.at[tuple(place)].set(largest)


def levels(key, extent, cuts, low, top_value):
    def one(dim, parts):
        heights = jax.random.uniform(jax.random.fold_in(jax.random.fold_in(key, 6), dim), (parts,), jnp.float32, low / len(cuts), top_value / len(cuts))
        return jnp.repeat(jnp.exp(heights), extent[dim] // parts).reshape((-1,) + (1,) * (len(extent) - dim - 1))

    level = one(*cuts[0])
    for cut in cuts[1:]:
        level = level * one(*cut)
    return level


def gaussian(own_key, shape, scale, reach, cuts=(), kind=jnp.bfloat16):
    factor_of = levels(own_key, shape, cuts, -0.22, 0.18) if cuts else 1.0
    drawn = jax.random.normal(own_key, shape, jnp.float32) * scale * factor_of
    return jnp.minimum(jnp.maximum(drawn, -reach), reach).astype(kind)


def setup_inputs(seed: int = 0) -> dict:
    key_of = jax.random.split(jax.random.key(seed), 9)
    right_side = draw_right_side(jax.random.fold_in(key_of[8], 71), 0)
    start_field = gaussian(key_of[1], (2, 3, S, NZ, NX, NY), 0.3, 1.75, ((3, 16), (4, 2)), jnp.float32)
    region = with_ends(jax.random.randint(key_of[2], (NZ, NX, NY), 0, NREG), jax.random.fold_in(key_of[2], 1), 0, NREG - 1).astype(jnp.int32)
    core_mask = with_ends((jax.random.randint(key_of[3], (NZ, NX, NY), 0, 3) < 1).astype(jnp.int32), jax.random.fold_in(key_of[3], 1), 0, 1)
    intensity = jnp.clip(4.0 * jax.random.uniform(key_of[4], (NZ, NX, NY), jnp.float32) ** levels(key_of[4], (NZ, NX, NY), ((0, 16), (1, 2)), -0.2, 0.2), 0.0, 4.0)
    eps_lin = jnp.clip(jax.random.uniform(key_of[5], (NREG,), jnp.float32, 1.0, 12.0), 1.0, 12.0)
    eps_loss = jnp.clip(jnp.exp(jax.random.uniform(key_of[6], (NREG,), jnp.float32, math.log(0.1), math.log(3.0))), 0.1, 3.0)
    kerr_coef = jnp.clip(jax.random.uniform(key_of[7], (NREG,), jnp.float32, 0.2, 1.0), 0.2, 1.0)
    return dict(right_side=right_side, start_field=start_field, region=region, core_mask=core_mask, intensity=intensity, eps_lin=eps_lin, eps_loss=eps_loss, kerr_coef=kerr_coef)


wave_sq = 0.25
wave_shift = 0.02
loss_gain = 3.2
tiny = 1e-6


def trimmed(values, direction):
    selector = [slice(None)] * (values.ndim - 3) + [slice(0, -1)] * 3
    if direction is not None:
        selector[values.ndim + direction] = slice(1, None)
    return values[tuple(selector)]


def advance(values, direction):
    return trimmed(values, direction) - trimmed(values, None)


def upper(values, direction):
    selector = [slice(None)] * (values.ndim - 3) + [slice(1, None)] * 3
    if direction is not None:
        selector[values.ndim + direction] = slice(0, -1)
    return values[tuple(selector)]


def retreat(values, direction):
    return upper(values, None) - upper(values, direction)


def curl_twice(padded):
    field_x = padded[:, 0]
    field_y = padded[:, 1]
    field_z = padded[:, 2]
    magnet_x = advance(field_z, -1) - advance(field_y, -3)
    magnet_y = advance(field_x, -3) - advance(field_z, -2)
    magnet_z = advance(field_y, -2) - advance(field_x, -1)
    result_x = retreat(magnet_z, -1) - retreat(magnet_y, -3)
    result_y = retreat(magnet_x, -3) - retreat(magnet_z, -2)
    result_z = retreat(magnet_y, -2) - retreat(magnet_x, -1)
    return jnp.stack([result_x, result_y, result_z], axis=1)


def apply_operator(values, padded, perm_real, perm_imag):
    curled = curl_twice(padded)
    real_part = values[0]
    imag_part = values[1]
    out_real = curled[0] - wave_sq * (perm_real * real_part - perm_imag * imag_part)
    out_imag = curled[1] - wave_sq * (perm_real * imag_part + perm_imag * real_part)
    return jnp.stack([out_real, out_imag])


def descend(gain_real, gain_imag, previous, plane_real, plane_imag, source):
    denom_real = plane_real - gain_real
    denom_imag = plane_imag - gain_imag
    magnitude = denom_real * denom_real + denom_imag * denom_imag
    new_real = denom_real / magnitude
    new_imag = -denom_imag / magnitude
    sum_real = source[0] + previous[0]
    sum_imag = source[1] + previous[1]
    updated = jnp.stack([new_real * sum_real - new_imag * sum_imag, new_real * sum_imag + new_imag * sum_real])
    return new_real, new_imag, updated


def ascend(gain_real, gain_imag, forward_value, behind):
    return jnp.stack([forward_value[0] + gain_real * behind[0] - gain_imag * behind[1],
                      forward_value[1] + gain_real * behind[1] + gain_imag * behind[0]])


def solve_lines(right_part, diag_real, diag_imag, unroll_count):
    along_first = jnp.moveaxis(right_part, -3, 0)
    diag_rows_real = jnp.moveaxis(diag_real, -3, 0)
    diag_rows_imag = jnp.moveaxis(diag_imag, -3, 0)

    def downward(carried, element):
        gain_real, gain_imag, previous = carried
        plane_real, plane_imag, source = element
        gain_real, gain_imag, previous = descend(gain_real, gain_imag, previous, plane_real, plane_imag, source)
        return (gain_real, gain_imag, previous), (gain_real, gain_imag, previous)

    initial = (jnp.zeros_like(diag_rows_real[0]), jnp.zeros_like(diag_rows_real[0]), jnp.zeros_like(along_first[0]))
    unused, (gains_real, gains_imag, fronts) = lax.scan(downward, initial, (diag_rows_real, diag_rows_imag, along_first), unroll=unroll_count)

    def upward(behind, element):
        gain_real, gain_imag, forward_value = element
        new_value = ascend(gain_real, gain_imag, forward_value, behind)
        return new_value, new_value

    unused, values = lax.scan(upward, jnp.zeros_like(along_first[0]), (gains_real, gains_imag, fronts), reverse=True, unroll=unroll_count)
    return jnp.moveaxis(values, 0, -3)


def pad_grid(values):
    return jnp.pad(values, [(0, 0)] * (values.ndim - 3) + [(1, 1)] * 3)


def reference(right_side, start_field, region, core_mask, intensity, eps_lin, eps_loss, kerr_coef):
    perm_real = eps_lin[region] + core_mask.astype(jnp.float32) * kerr_coef[region] * intensity
    perm_imag = eps_loss[region]
    diag_real = 2.0 - wave_shift * perm_real
    diag_imag = (loss_gain / NZ) * perm_imag

    def solve_column(columns):
        right_part, initial = columns
        residual = right_part - apply_operator(initial, pad_grid(initial), perm_real, perm_imag)
        precond = solve_lines(residual, diag_real, diag_imag, 1)
        image_field = apply_operator(precond, pad_grid(precond), perm_real, perm_imag)
        cross_sum = jnp.sum(residual * image_field)
        self_sum = jnp.sum(image_field * image_field)
        return initial + (cross_sum / (self_sum + tiny)) * precond

    updated = lax.map(solve_column, (jnp.moveaxis(right_side, 2, 0), jnp.moveaxis(start_field, 2, 0)))
    return jnp.moveaxis(updated, 0, 2)
```

```python
import functools

import jax
import jax.numpy as jnp
from jax import lax
from jax.experimental import pallas as pl
from jax.experimental.pallas import tpu as pltpu
from jax.sharding import PartitionSpec as P

wave_sq = 0.25
wave_shift = 0.02
loss_gain = 3.2
tiny = 1e-06
MESH = pl.DeviceIdType.MESH


def cmul(a, b):
    return (a[0] * b[0] - a[1] * b[1], a[0] * b[1] + a[1] * b[0])


def cadd(a, b):
    return (a[0] + b[0], a[1] + b[1])


def csub(a, b):
    return (a[0] - b[0], a[1] - b[1])


def cneg(a):
    return (-a[0], -a[1])


def crecip(a):
    magnitude = a[0] * a[0] + a[1] * a[1]
    return (a[0] / magnitude, -a[1] / magnitude)


def strides(size):
    found = []
    d = 1
    while d < size:
        found.append(d)
        d *= 2
    return found


def shift_y(values, step):
    shape = values.shape
    flat = values.reshape((-1, shape[-1]))
    width = shape[-1]
    lane = lax.broadcasted_iota(jnp.int32, flat.shape, 1)
    rolled = pltpu.roll(flat, (-step) % width, 1)
    keep = lane < width - 1 if step == 1 else lane > 0
    return jnp.where(keep, rolled, 0.0).reshape(shape)


def curl_part(ext, q, nz, nx):
    def at(c, dz=0, dx=0):
        return ext[q, c, 1 + dz : 1 + dz + nz, 1 + dx : 1 + dx + nx]

    ux, uy, uz = at(0), at(1), at(2)
    ux_up, ux_down = shift_y(ux, 1), shift_y(ux, -1)
    uy_down = shift_y(uy, -1)
    uz_up, uz_down = shift_y(uz, 1), shift_y(uz, -1)
    dfx_y = at(1, 0, 1) - uy
    mixed = (dfx_y - shift_y(dfx_y, -1)) + ((at(2, 0, 1) - uz) - (at(2, -1, 1) - at(2, -1)))
    out_x = (ux - ux_up) + (ux - ux_down) + (ux - at(0, 1)) + (ux - at(0, -1)) + mixed
    ux_left = at(0, 0, -1)
    uz_back = at(2, -1)
    mixed = ((ux_up - ux) - (shift_y(ux_left, 1) - ux_left)) + ((uz_up - uz) - (shift_y(uz_back, 1) - uz_back))
    out_y = (uy - at(1, 0, 1)) + (uy - at(1, 0, -1)) + (uy - at(1, 1)) + (uy - at(1, -1)) + mixed
    dfz_y = at(1, 1) - uy
    mixed = ((at(0, 1) - ux) - (at(0, 1, -1) - ux_left)) + (dfz_y - shift_y(dfz_y, -1))
    out_z = (uz - at(2, 0, 1)) + (uz - at(2, 0, -1)) + (uz - uz_up) + (uz - uz_down) + mixed
    return (out_x, out_y, out_z)


def kernel(lat_n, prop_n, total_planes, right, field, region, mask, intensity, lin, loss, kerr, out,
           ext, ext2, resid, send_f, recv_f, send_c, recv_c, edge_f, edge_c, edge_y, sums, send_sem, recv_sem):
    parts, comps, nz, nx = field.shape[:4]
    sizes = {"lat": lat_n, "prop": prop_n}
    place = {name: lax.axis_index(name) for name in sizes}
    barrier = pltpu.get_barrier_semaphore()
    expected = jnp.int32(0)
    for name, size in sizes.items():
        me = place[name]
        for d in strides(size):
            for ok, peer in ((me >= d, me - d), (me + d < size, me + d)):
                @pl.when(ok)
                def _(name=name, peer=peer):
                    pl.semaphore_signal(barrier, inc=1, device_id={name: peer}, device_id_type=MESH)
                expected = expected + ok.astype(jnp.int32)
    used = [0]
    pending = []

    def send(name, d, upward, src, dst):
        number = used[0]
        used[0] += 1
        me, size = place[name], sizes[name]
        below, above = me >= d, me + d < size
        goes, comes = (above, below) if upward else (below, above)
        peer = me + d if upward else me - d

        def copy():
            return pltpu.make_async_remote_copy(
                src_ref=src, dst_ref=dst, send_sem=send_sem.at[number], recv_sem=recv_sem.at[number],
                device_id={name: peer}, device_id_type=MESH)

        @pl.when(goes)
        def _():
            copy().start()

        pending.append((goes, copy))

        def arrive():
            @pl.when(comes)
            def _():
                copy().wait_recv()

        return arrive

    def clear(ok, ref):
        @pl.when(ok)
        def _():
            ref[...] = jnp.zeros(ref.shape, jnp.float32)

    k, j = place["prop"], place["lat"]
    first, last = k == 0, k == prop_n - 1
    clear(first, ext.at[:, :, 0, 1 : 1 + nx])
    clear(last, ext.at[:, :, nz + 1, 1 : 1 + nx])
    for target in (ext, ext2):
        clear(j == 0, target.at[:, :, :, 0])
        clear(j == lat_n - 1, target.at[:, :, :, nx + 1])
    clear(last, edge_f)
    clear(last, edge_c)
    clear(first, edge_y)
    for index, d in enumerate(strides(prop_n)):
        for side, empty in ((0, k < d), (1, k + d >= prop_n)):
            clear(empty, recv_f.at[index, side])
            clear(empty, recv_c.at[index, side])

    pl.semaphore_wait(barrier, expected)

    def swap_x(target):
        a = send("lat", 1, True, target.at[:, :, :, nx], target.at[:, :, :, 0])
        b = send("lat", 1, False, target.at[:, :, :, 1], target.at[:, :, :, nx + 1])
        return a, b

    arrive_a = send("prop", 1, True, field.at[:, :, nz - 1], ext.at[:, :, 0, 1 : 1 + nx])
    arrive_b = send("prop", 1, False, field.at[:, :, 0], ext.at[:, :, nz + 1, 1 : 1 + nx])
    for q in range(parts):
        ext[q, :, 1 : 1 + nz, 1 : 1 + nx] = field[q]

    cells = region[...]
    lin_cell = loss_cell = kerr_cell = jnp.zeros(cells.shape, jnp.float32)
    for level in range(lin.shape[0]):
        hit = cells == level
        lin_cell = jnp.where(hit, lin[level], lin_cell)
        loss_cell = jnp.where(hit, loss[level], loss_cell)
        kerr_cell = jnp.where(hit, kerr[level], kerr_cell)
    perm_real = lin_cell + mask[...].astype(jnp.float32) * kerr_cell * intensity[...]
    diag_real = 2.0 - wave_shift * perm_real
    diag_imag = (loss_gain / total_planes) * loss_cell
    diag = [(diag_real[z], diag_imag[z]) for z in range(nz)]
    inner = nz - 1
    gains = []
    for z in range(inner):
        gains.append(crecip(diag[z] if z == 0 else csub(diag[z], gains[-1])))
    low = [gains[0]]
    for z in range(1, inner):
        low.append(cmul(gains[z], low[-1]))
    for z in range(inner - 2, -1, -1):
        low[z] = cadd(low[z], cmul(gains[z], low[z + 1]))
    high = [None] * inner
    high[inner - 1] = gains[inner - 1]
    for z in range(inner - 2, -1, -1):
        high[z] = cmul(gains[z], high[z + 1])

    arrive_a()
    arrive_b()
    for arrive in swap_x(ext):
        arrive()

    def operate(source, q, curled, c):
        here = source[q, c, 1 : 1 + nz, 1 : 1 + nx]
        other = source[1 - q, c, 1 : 1 + nz, 1 : 1 + nx]
        if q == 0:
            return curled - wave_sq * (perm_real * here - loss_cell * other)
        return curled - wave_sq * (perm_real * here + loss_cell * other)

    for q in range(parts):
        curled = curl_part(ext, q, nz, nx)
        for c in range(comps):
            resid[q, c] = right[q, c] - operate(ext, q, curled[c], c)

    def res(z):
        return (resid[0, :, z], resid[1, :, z])

    locals_ = [cmul(gains[0], res(0))]
    for z in range(1, inner):
        locals_.append(cmul(gains[z], cadd(res(z), locals_[-1])))
    for z in range(inner - 2, -1, -1):
        locals_[z] = cadd(locals_[z], cmul(gains[z], locals_[z + 1]))
    steps = strides(prop_n)
    count = len(steps)
    for q in range(parts):
        send_f[count, q] = locals_[0][q]
        send_c[count, q, 0] = low[0][q]
        send_c[count, q, 1] = low[inner - 1][q]
    arrive_a = send("prop", 1, False, send_f.at[count], edge_f)
    arrive_b = send("prop", 1, False, send_c.at[count], edge_c)
    for z in range(inner):
        for q in range(parts):
            ext2[q, :, 1 + z, 1 : 1 + nx] = locals_[z][q]
    partial = cadd(res(nz - 1), locals_[inner - 1])
    arrive_a()
    arrive_b()
    inverse = crecip(csub(csub(diag[nz - 1], high[inner - 1]), (edge_c[0, 0], edge_c[1, 0])))
    below = cneg(cmul(low[inner - 1], inverse))
    above = cneg(cmul((edge_c[0, 1], edge_c[1, 1]), inverse))
    value = cmul(inverse, cadd(partial, (edge_f[0], edge_f[1])))
    for index, d in enumerate(steps):
        for q in range(parts):
            send_f[index, q] = value[q]
            send_c[index, q, 0] = below[q]
            send_c[index, q, 1] = above[q]
        arrivals = []
        for side, upward in ((0, True), (1, False)):
            arrivals.append(send("prop", d, upward, send_c.at[index], recv_c.at[index, side]))
            arrivals.append(send("prop", d, upward, send_f.at[index], recv_f.at[index, side]))
        for arrive in arrivals:
            arrive()

        def coef(side, which):
            return (recv_c[index, side, 0, which], recv_c[index, side, 1, which])

        drop = cadd(cmul(below, coef(0, 1)), cmul(above, coef(1, 0)))
        inverse = crecip((1.0 - drop[0], -drop[1]))
        lower = cmul(below, inverse)
        upper = cmul(above, inverse)
        value = csub(
            cmul(inverse, value),
            cadd(cmul(lower, (recv_f[index, 0, 0], recv_f[index, 0, 1])),
                 cmul(upper, (recv_f[index, 1, 0], recv_f[index, 1, 1]))))
        below = cneg(cmul(lower, coef(0, 0)))
        above = cneg(cmul(upper, coef(1, 1)))

    for q in range(parts):
        send_f[count + 1, q] = value[q]
        ext2[q, :, nz, 1 : 1 + nx] = value[q]
    send("prop", 1, True, send_f.at[count + 1], edge_y)()
    before = (edge_y[0], edge_y[1])
    solved = None
    for z in range(inner):
        mine = (ext2[0, :, 1 + z, 1 : 1 + nx], ext2[1, :, 1 + z, 1 : 1 + nx])
        solved = cadd(mine, cadd(cmul(low[z], before), cmul(high[z], value)))
        for q in range(parts):
            ext2[q, :, 1 + z, 1 : 1 + nx] = solved[q]
    after = csub(csub(cmul(diag[nz - 1], value), solved), res(nz - 1))
    for q in range(parts):
        ext2[q, :, 0, 1 : 1 + nx] = before[q]
        ext2[q, :, nz + 1, 1 : 1 + nx] = jnp.where(last, 0.0, after[q])
    for arrive in swap_x(ext2):
        arrive()

    cross = own = jnp.zeros(field.shape[-2:], jnp.float32)
    for q in range(parts):
        curled = curl_part(ext2, q, nz, nx)
        for c in range(comps):
            image = operate(ext2, q, curled[c], c)
            cross = cross + jnp.sum(resid[q, c] * image, axis=(0, 1))
            own = own + jnp.sum(image * image, axis=(0, 1))
    lane = lax.broadcasted_iota(jnp.int32, cross.shape, 1)
    half = cross.shape[1] // 2
    total = jnp.where(lane < half, jnp.sum(cross, axis=1, keepdims=True), jnp.sum(own, axis=1, keepdims=True))
    turn = 0
    for name, size in sizes.items():
        me = place[name]
        for d in strides(size):
            sums[turn, 0] = total
            upper_half = lax.rem(me // d, 2) == 1
            peer = jnp.where(upper_half, me - d, me + d)
            number = used[0]
            used[0] += 1
            copy = pltpu.make_async_remote_copy(
                src_ref=sums.at[turn, 0], dst_ref=sums.at[turn, 1], send_sem=send_sem.at[number],
                recv_sem=recv_sem.at[number], device_id={name: peer}, device_id_type=MESH)
            copy.start()
            copy.wait()
            total = total + sums[turn, 1]
            turn += 1
    step_size = total[:, 0:1] / (total[:, half : half + 1] + tiny)
    for q in range(parts):
        for c in range(comps):
            out[q, c] = field[q, c] + step_size * ext2[q, c, 1 : 1 + nz, 1 : 1 + nx]
    for goes, copy in pending:
        @pl.when(goes)
        def _(copy=copy):
            copy().wait_send()


def per_device(lat_n, prop_n, right_side, start_field, region, core_mask, intensity, eps_lin, eps_loss, kerr_coef):
    order = (0, 1, 3, 4, 2, 5)
    right = jnp.transpose(right_side, order)
    field = jnp.transpose(start_field, order)
    parts, comps, nz, nx, columns, ny = field.shape
    steps = len(strides(prop_n))
    turns = steps + len(strides(lat_n))
    plane = (parts, comps, nx, columns, ny)
    coefs = (parts, 2, nx, 1, ny)
    cells = (nz, nx, 1, ny)
    sem_count = 16 + 4 * steps + turns
    f32 = functools.partial(pltpu.VMEM, dtype=jnp.float32)
    vmem = pl.BlockSpec(memory_space=pltpu.VMEM)
    smem = pl.BlockSpec(memory_space=pltpu.SMEM)
    extended = (parts, comps, nz + 2, nx + 2, columns, ny)
    out = pl.pallas_call(
        functools.partial(kernel, lat_n, prop_n, nz * prop_n),
        out_shape=jax.ShapeDtypeStruct(field.shape, jnp.float32),
        in_specs=[vmem] * 5 + [smem] * 3,
        out_specs=vmem,
        scratch_shapes=[
            f32(extended), f32(extended), f32(field.shape),
            f32((steps + 2,) + plane), f32((steps, 2) + plane),
            f32((steps + 1,) + coefs), f32((steps, 2) + coefs),
            f32(plane), f32(coefs), f32(plane),
            f32((turns, 2, columns, ny)),
            pltpu.SemaphoreType.DMA((sem_count,)), pltpu.SemaphoreType.DMA((sem_count,)),
        ],
        compiler_params=pltpu.CompilerParams(collective_id=0, has_side_effects=True),
    )(right, field, region.reshape(cells), core_mask.reshape(cells), intensity.reshape(cells), eps_lin, eps_loss, kerr_coef)
    return jnp.transpose(out, (0, 1, 4, 2, 3, 5))


def solution(mesh):
    field = P(None, None, None, "prop", "lat", None)
    cell = P("prop", "lat", None)
    return jax.shard_map(
        functools.partial(per_device, mesh.shape["lat"], mesh.shape["prop"]),
        mesh=mesh,
        in_specs=(field, field, cell, cell, cell, P(), P(), P()),
        out_specs=field,
        check_vma=False,
    )
```
